512 devices in a mesh: mom: 8 (over y, x_lo), shard: 64 (over x_hi, z, core).
Axes of the slice: x: 4 (x_hi: 2, x_lo: 2; x = x_hi * 2 + x_lo), y: 4, z: 16, core: 2. Of those that a mesh axis runs over, the one named last changes fastest.
Arguments:
- green_ret: bfloat16 [8, 256, 8, 2, 128, 128], P('mom', 'shard'), may hold values from -4 to 4
- broadening: bfloat16 [2, 128, 128], replicated, may hold values from -0.5 to 0.5
- occupation: float32 [8, 256], P('mom', 'shard'), may hold values from 0.1 to 1
- neighbours: int32 [64, 4], replicated, may hold values from 0 to 63, as said below
- orbitals: int32 [64], replicated, may hold values from 4 to 16
- coupling: bfloat16 [64, 4, 256, 256], P('shard'), may hold values from -0.1875 to 0.1875
- phonon: float32 [8, 2, 256], replicated, may hold values from -5 to 5
- mode_table: int32 [8, 8], replicated, may hold values from 0 to 7, as said below
Outputs:
- self_energy: bfloat16 [8, 256, 64, 2, 256], P('mom', None, 'shard')
The draws below stay inside these ranges and needn't reach their ends.
Inputs may be any that keep to these rules, and one draw needn't show every extreme that they name: `neighbours`: row a holds 4 distinct atoms of a's own layer block (atoms 8 * (a // 8) onward), none equal to a; the first is a with its lowest bit flipped. `mode_table`: each entry names one of the 8 phonon modes.
All inputs are finite; a program needn't handle non-finite values.
Results may differ from the reference program's by a relative error of at most 0.013.
Values may be sent and summed in bfloat16 or wider, within the bound.
No kernel may reach another device: no remote copies, remote signals or barrier semaphores. Data moves between devices by JAX's collectives and lax.ppermute only.
A program may use at most 192 MiB of HBM per device.

```python
import math
import jax
import jax.numpy as jnp
import numpy as np
from jax import lax

NORB = 16
ATL = 8
NBR = 4
MODES = 8
ENERGIES = 256
LAYERS = 8
ORB = 128
PAIR = 256
ATOMS = 64
KPTS = 8


def draw_neighbours(key, part):
    candidate_rows = np.array([[column_slot for column_slot in range(ATL) if column_slot != atom_slot and column_slot != atom_slot ^ 1] for atom_slot in range(ATL)], dtype=np.int32)
    atom_ids = jnp.arange(ATOMS, dtype=jnp.int32)
    in_layer = atom_ids % ATL
    layer_start = atom_ids - in_layer
    candidates = jnp.asarray(candidate_rows)[in_layer]
    scores = jax.random.randint(key, (ATOMS, ATL - 2), 0, 1 << 20, dtype=jnp.int32) * (ATL - 2) + jnp.arange(ATL - 2, dtype=jnp.int32)[None, :]
    ordering = jnp.argsort(scores, axis=1)
    chosen = jnp.take_along_axis(candidates, ordering[:, :NBR - 1], axis=1)
    partner = layer_start + jnp.bitwise_xor(in_layer, 1)
    return jnp.concatenate([partner[:, None], layer_start[:, None] + chosen], axis=1).astype(jnp.int32)


def draw_mode_table(key, part):
    table_key = jax.random.fold_in(key, 7)
    drawn = jax.random.randint(table_key, (KPTS, KPTS), 0, MODES, dtype=jnp.int32)
    row_ids = jnp.arange(KPTS, dtype=jnp.int32)[:, None]
    column_ids = jnp.arange(KPTS, dtype=jnp.int32)[None, :]
    pinned = (row_ids == KPTS - 1) & (column_ids == 0)
    return jnp.where(pinned, MODES - 1, drawn).astype(jnp.int32)


def set_ends(values, own_key, smallest, high):
    spot = [jax.random.randint(jax.random.fold_in(own_key, axis), (), 0, length) for axis, length in enumerate(values.shape)]
    longest = values.shape.index(max(values.shape))
    next_to = spot[:longest] + [(spot[longest] + 1) % values.shape[longest]] + spot[longest + 1:]
    return values.at[tuple(spot)].set(smallest).at[tuple(next_to)].set(high)


def block_scale(own_key, extent, cuts, least, high):
    gain = 1.0
    for position, parts in cuts:
        heights = jax.random.uniform(jax.random.fold_in(jax.random.fold_in(own_key, 6), position), (parts,), jnp.float32, least / len(cuts), high / len(cuts))
        gain = gain * jnp.repeat(jnp.exp(heights), extent[position] // parts).reshape((-1,) + (1,) * (len(extent) - 1 - position))
    return gain


def bell_draw(rng, extent, deviation, bound, split=(), kind=jnp.bfloat16):
    gain = block_scale(rng, extent, split, -0.22, 0.18) if split else 1.0
    values = jax.random.normal(rng, extent, jnp.float32) * deviation * gain
    return jnp.minimum(jnp.maximum(values, -bound), bound).astype(kind)


def setup_inputs(seed: int = 0) -> dict:
    seeds = jax.random.split(jax.random.key(seed), 9)
    return {
        "green_ret": bell_draw(seeds[0], (KPTS, ENERGIES, LAYERS, 2, ORB, ORB), 0.3, 4.0, ((0, 8), (1, 64))),
        "broadening": bell_draw(seeds[1], (2, ORB, ORB), ORB ** -0.5, 0.5),
        "occupation": jnp.clip(0.1 + 0.9 * jax.random.uniform(seeds[2], (KPTS, ENERGIES), jnp.float32) ** block_scale(seeds[2], (KPTS, ENERGIES), ((0, 8), (1, 64)), -0.2, 0.2), 0.1, 1.0),
        "neighbours": draw_neighbours(jax.random.fold_in(seeds[8], 71), 0),
        "orbitals": set_ends(jax.random.randint(seeds[4], (ATOMS,), NORB // 4, NORB + 1), jax.random.fold_in(seeds[4], 1), NORB // 4, NORB).astype(jnp.int32),
        "coupling": bell_draw(seeds[5], (ATOMS, NBR, PAIR, PAIR), (NBR * PAIR) ** -0.5, 0.1875, ((0, 64),)),
        "phonon": bell_draw(seeds[6], (MODES, 2, ENERGIES), 0.7, 5.0, (), jnp.float32),
        "mode_table": draw_mode_table(jax.random.fold_in(seeds[8], 71), 0),
    }


def dft_tables(length):
    counter = jnp.arange(length, dtype=jnp.int32)
    phases = (counter[:, None] * counter[None, :]) % length
    angles = phases.astype(jnp.float32) * (2.0 * math.pi / length)
    return jnp.cos(angles).astype(jnp.bfloat16), jnp.sin(angles).astype(jnp.bfloat16)


def settle(values):
    return lax.optimization_barrier(values.astype(jnp.bfloat16)).astype(jnp.float32)


def coupled_block(green_block, occupation_block, broadening, neighbours, orbitals, coupling):
    block_len = green_block.shape[0]
    highest = lax.Precision.HIGHEST
    stacked = jnp.concatenate([broadening[0], broadening[1]], axis=1)
    products = jnp.dot(green_block.reshape(-1, ORB), stacked, preferred_element_type=jnp.float32)
    products = products.reshape(block_len, LAYERS, 2, ORB, 2, ORB)
    left_re = settle(products[:, :, 0, :, 0] - products[:, :, 1, :, 1])
    left_im = settle(products[:, :, 0, :, 1] + products[:, :, 1, :, 0])
    green_full = green_block.astype(jnp.float32)
    green_re = green_full[:, :, 0]
    green_im = green_full[:, :, 1]
    full_re = jnp.einsum('elik,eljk->elij', left_re, green_re, precision=highest) + jnp.einsum('elik,eljk->elij', left_im, green_im, precision=highest)
    full_im = jnp.einsum('elik,eljk->elij', left_im, green_re, precision=highest) - jnp.einsum('elik,eljk->elij', left_re, green_im, precision=highest)
    weight = occupation_block[:, None, None, None]
    stacked_full = jnp.stack([full_re * weight, full_im * weight], axis=2)
    blocks = stacked_full.reshape(block_len, LAYERS, 2, ATL, NORB, ATL, NORB)
    blocks = blocks.transpose(0, 1, 3, 5, 2, 4, 6).reshape(block_len, ATOMS, ATL, 2, NORB, NORB)
    slot_atoms = neighbours % ATL
    chosen = jnp.take_along_axis(blocks, slot_atoms[None, :, :, None, None, None], axis=2)
    counter = jnp.arange(NORB, dtype=jnp.int32)
    row_mask = counter[None, :] < orbitals[:, None]
    column_mask = counter[None, None, :] < orbitals[neighbours][:, :, None]
    pair_mask = (row_mask[:, None, :, None] & column_mask[:, :, None, :]).astype(jnp.float32)
    scaled = chosen * pair_mask[None, :, :, None, :, :]
    pair_blocks = settle(scaled.reshape(block_len, ATOMS, NBR, 2, PAIR))
    mixed_terms = jnp.einsum('eanpx,anxy->eapy', pair_blocks, coupling.astype(jnp.float32), precision=highest)
    pair_index = jnp.arange(PAIR, dtype=jnp.int32)
    own_mask = ((pair_index[None, :] // NORB < orbitals[:, None]) & (pair_index[None, :] % NORB < orbitals[:, None])).astype(jnp.float32)
    return (mixed_terms * own_mask[None, :, None, :]).astype(jnp.bfloat16)


def reference(green_ret, broadening, occupation, neighbours, orbitals, coupling, phonon, mode_table):
    cos_table, sin_table = dft_tables(ENERGIES)
    block_len = math.gcd(ENERGIES, 64)
    block_count = ENERGIES // block_len

    def per_momentum(inputs):
        green_one, occupation_one = inputs

        def one_block(block_in):
            return coupled_block(block_in[0], block_in[1], broadening, neighbours, orbitals, coupling)

        coupled = lax.map(one_block, (green_one.reshape(block_count, block_len, LAYERS, 2, ORB, ORB), occupation_one.reshape(block_count, block_len)))
        flat_coupled = coupled.reshape(ENERGIES, -1)
        part_cos = jnp.dot(cos_table, flat_coupled, preferred_element_type=jnp.float32).reshape(ENERGIES, ATOMS, 2, PAIR)
        part_sin = jnp.dot(sin_table, flat_coupled, preferred_element_type=jnp.float32).reshape(ENERGIES, ATOMS, 2, PAIR)
        timed_re = part_cos[:, :, 0] + part_sin[:, :, 1]
        timed_im = part_cos[:, :, 1] - part_sin[:, :, 0]
        return jnp.stack([timed_re, timed_im], axis=2).astype(jnp.bfloat16)

    time_data = lax.map(per_momentum, (green_ret, occupation))
    time_values = lax.optimization_barrier(time_data).astype(jnp.float32)

    def per_target(target_index):
        kernel = phonon[mode_table[target_index]]
        kernel_re = kernel[:, 0][:, :, None, None]
        kernel_im = kernel[:, 1][:, :, None, None]
        sum_re = jnp.sum(kernel_re * time_values[:, :, :, 0] - kernel_im * time_values[:, :, :, 1], axis=0)
        sum_im = jnp.sum(kernel_re * time_values[:, :, :, 1] + kernel_im * time_values[:, :, :, 0], axis=0)
        convolved = jnp.stack([sum_re, sum_im], axis=2).astype(jnp.bfloat16)
        flat_conv = convolved.reshape(ENERGIES, -1)
        back_cos = jnp.dot(cos_table, flat_conv, preferred_element_type=jnp.float32).reshape(ENERGIES, ATOMS, 2, PAIR)
        back_sin = jnp.dot(sin_table, flat_conv, preferred_element_type=jnp.float32).reshape(ENERGIES, ATOMS, 2, PAIR)
        out_re = (back_cos[:, :, 0] - back_sin[:, :, 1]) * (1.0 / ENERGIES)
        out_im = (back_cos[:, :, 1] + back_sin[:, :, 0]) * (1.0 / ENERGIES)
        return jnp.stack([out_re, out_im], axis=2).astype(jnp.bfloat16)

    return lax.map(per_target, jnp.arange(KPTS, dtype=jnp.int32))
```

```python
import functools

import jax
import jax.numpy as jnp
import numpy as np
from jax import lax
from jax.experimental import pallas as pl
from jax.experimental.pallas import tpu as pltpu
from jax.sharding import PartitionSpec as P

NORB = 16
ATL = 8
NBR = 4
ENERGIES = 256
LAYERS = 8
ORB = 128
PAIR = 256
ATOMS = 64
KPTS = 8
CHUNKS = 1

F32 = jnp.float32
BF16 = jnp.bfloat16
VMEM_SPEC = pl.BlockSpec(memory_space=pltpu.VMEM)


def dft_tables(length):
    counter = np.arange(length)
    angles = (counter[:, None] * counter[None, :] % length) * (2.0 * np.pi / length)
    return np.cos(angles).astype(jnp.bfloat16), np.sin(angles).astype(jnp.bfloat16)


def pairs_kernel(first, occ_ref, nbr_ref, orb_ref, green_ref, mix_ref, out_ref):
    layer = pl.program_id(0)
    energies = green_ref.shape[1]
    rows = []
    for e in range(energies):
        rows.append(jnp.concatenate([green_ref[0, e, 0, 0], green_ref[0, e, 0, 1]], axis=1))
    left = jnp.dot(jnp.concatenate(rows, axis=0), mix_ref[...], preferred_element_type=F32)
    left = left.astype(BF16)
    full = []
    for e in range(energies):
        green_re = green_ref[0, e, 0, 0]
        green_im = green_ref[0, e, 0, 1]
        partner = jnp.concatenate(
            [
                jnp.concatenate([green_re, green_im], axis=1),
                jnp.concatenate([-green_im, green_re], axis=1),
            ],
            axis=0,
        )
        block = lax.dot_general(
            left[e * ORB : (e + 1) * ORB],
            partner,
            (((1,), (1,)), ((), ())),
            preferred_element_type=F32,
        )
        full.append((block * occ_ref[0, first + e]).astype(BF16))
    lane = lax.broadcasted_iota(jnp.int32, (1, ORB), 1)
    slot = (lane // NORB) % NBR
    column = lane % NORB
    source = lax.broadcasted_iota(jnp.int32, (ORB, ORB), 0)
    row = lax.broadcasted_iota(jnp.int32, (energies * NORB, ORB), 0) % NORB
    low = lax.broadcasted_iota(jnp.int32, (energies * NORB, ORB), 1) < ORB // 2
    for a in range(ATL):
        atom = layer * ATL + a
        target = jnp.full((1, ORB), -1, jnp.int32)
        for n in range(NBR):
            partner_atom = nbr_ref[atom, n]
            start = (partner_atom % ATL) * NORB
            chosen = (slot == n) & (column < orb_ref[partner_atom])
            target = jnp.where(chosen, start + column, target)
        select = jnp.where(source == target, 1.0, 0.0).astype(BF16)
        part_rows = [
            full[e][a * NORB : (a + 1) * NORB, p * ORB : (p + 1) * ORB]
            for p in range(2)
            for e in range(energies)
        ]
        picked = jnp.dot(jnp.concatenate(part_rows, axis=0), select, preferred_element_type=F32)
        half = energies * NORB
        merged = jnp.where(low, picked[:half], picked[half:])
        merged = jnp.where(row < orb_ref[atom], merged, 0.0).astype(BF16)
        out_ref[a] = merged.reshape(energies, NORB, ORB)


def make_pairs(green_ret, mixing, occupation, neighbours, orbitals, chunk):
    energies = green_ret.shape[1] // CHUNKS
    smem = pl.BlockSpec(memory_space=pltpu.SMEM)
    return pl.pallas_call(
        functools.partial(pairs_kernel, chunk * energies),
        grid=(LAYERS,),
        in_specs=[
            smem,
            smem,
            smem,
            pl.BlockSpec((1, energies, 1, 2, ORB, ORB), lambda l: (0, chunk, l, 0, 0, 0)),
            pl.BlockSpec((2 * ORB, 2 * ORB), lambda l: (0, 0)),
        ],
        out_specs=pl.BlockSpec((ATL, energies, NORB, ORB), lambda l: (l, 0, 0, 0)),
        out_shape=jax.ShapeDtypeStruct((ATOMS, energies, NORB, ORB), BF16),
        name=f"pairs{chunk}",
    )(occupation, neighbours, orbitals, green_ret, mixing)


def couple_kernel(*refs):
    arrived, (weight_ref, mask_ref, table_ref, out_ref, wide) = refs[:CHUNKS], refs[CHUNKS:]
    per_chunk = arrived[0].shape[1]
    for chunk in range(CHUNKS):
        rows = arrived[chunk].shape[0] * per_chunk * NORB
        wide[chunk * rows : (chunk + 1) * rows] = (
            arrived[chunk][...].reshape(rows, ORB).astype(F32)
        )
    total = jnp.zeros((ENERGIES, 2 * PAIR), F32)
    for step in range(NORB // 2):
        rows = jnp.concatenate(
            [wide[pl.ds(2 * step + u, ENERGIES, stride=NORB), :].astype(BF16) for u in range(2)],
            axis=1,
        )
        total = total + jnp.dot(rows, weight_ref[step], preferred_element_type=F32)
    coupled = (total * mask_ref[...]).astype(BF16)
    spectra = jnp.dot(table_ref[...], coupled, preferred_element_type=F32)
    out_ref[:, :PAIR] = (spectra[:ENERGIES, :PAIR] + spectra[ENERGIES:, PAIR:]).astype(BF16)
    out_ref[:, PAIR:] = (spectra[:ENERGIES, PAIR:] - spectra[ENERGIES:, :PAIR]).astype(BF16)


def convolve_kernel(values_ref, kernel_ref, out_ref):
    for target in range(KPTS):
        sum_re = 0.0
        sum_im = 0.0
        for source in range(KPTS):
            column = (target * KPTS + source) * 2
            kernel_re = kernel_ref[:, column : column + 1]
            kernel_im = kernel_ref[:, column + 1 : column + 2]
            value_re = values_ref[source, :, :PAIR].astype(F32)
            value_im = values_ref[source, :, PAIR:].astype(F32)
            sum_re = sum_re + (kernel_re * value_re - kernel_im * value_im)
            sum_im = sum_im + (kernel_re * value_im + kernel_im * value_re)
        out_ref[target, :, :PAIR] = sum_re.astype(BF16)
        out_ref[target, :, PAIR:] = sum_im.astype(BF16)


def back_kernel(values_ref, table_ref, out_ref):
    values = jnp.concatenate([values_ref[:, :PAIR], values_ref[:, PAIR:]], axis=0)
    result = jnp.dot(table_ref[...], values, preferred_element_type=F32)
    out_ref[...] = (result * (1.0 / ENERGIES)).astype(BF16)


def local(
    green_ret, broadening, occupation, neighbours, orbitals, coupling, phonon, mode_table
):
    highest = lax.Precision.HIGHEST
    mixing = jnp.concatenate(
        [
            jnp.concatenate([broadening[0], broadening[1]], axis=1),
            jnp.concatenate([-broadening[1], broadening[0]], axis=1),
        ],
        axis=0,
    )
    arrived = []
    for chunk in range(CHUNKS):
        pairs = make_pairs(green_ret, mixing, occupation, neighbours, orbitals, chunk)
        arrived.append(lax.all_to_all(pairs, "shard", split_axis=0, concat_axis=0, tiled=True))

    parts = coupling.reshape(NBR, NORB, NORB, PAIR).transpose(1, 0, 2, 3)
    parts = parts.reshape(NORB, NBR * NORB, PAIR)
    zeros = jnp.zeros_like(parts)
    weights = jnp.concatenate(
        [
            jnp.concatenate([parts, zeros], axis=2),
            jnp.concatenate([zeros, parts], axis=2),
        ],
        axis=1,
    ).reshape(NORB // 2, 4 * NBR * NORB, 2 * PAIR)
    own_atom = lax.axis_index("shard")
    own_count = lax.dynamic_slice_in_dim(orbitals, own_atom, 1)[0]
    pair_index = jnp.arange(2 * PAIR, dtype=jnp.int32) % PAIR
    own_mask = (pair_index // NORB < own_count) & (pair_index % NORB < own_count)
    own_mask = own_mask.astype(F32)[None, :]
    cos_table, sin_table = dft_tables(ENERGIES)
    forward = jnp.asarray(np.concatenate([cos_table, sin_table], axis=0))
    timed = pl.pallas_call(
        couple_kernel,
        in_specs=[VMEM_SPEC] * (CHUNKS + 3),
        out_specs=VMEM_SPEC,
        out_shape=jax.ShapeDtypeStruct((ENERGIES, 2 * PAIR), BF16),
        scratch_shapes=[pltpu.VMEM((ENERGIES * NORB, ORB), F32)],
        name="couple",
    )(*arrived, weights, own_mask, forward)

    span = ENERGIES // KPTS
    own_momentum = lax.axis_index("mom")
    own_phonon = lax.dynamic_slice_in_dim(phonon, own_momentum * span, span, 2)
    mode_ids = jnp.arange(phonon.shape[0], dtype=jnp.int32)
    one_hot = (mode_table.reshape(-1, 1) == mode_ids[None, :]).astype(F32)
    kernel = jnp.dot(one_hot, own_phonon.reshape(phonon.shape[0], -1), precision=highest)
    kernel = kernel.reshape(KPTS * KPTS * 2, span).T

    moved = lax.all_to_all(
        timed.reshape(KPTS, span, 2 * PAIR), "mom", split_axis=0, concat_axis=0, tiled=True
    )
    convolved = pl.pallas_call(
        convolve_kernel,
        in_specs=[VMEM_SPEC] * 2,
        out_specs=VMEM_SPEC,
        out_shape=jax.ShapeDtypeStruct((KPTS, span, 2 * PAIR), BF16),
        name="convolve",
    )(moved, kernel)
    returned = lax.all_to_all(convolved, "mom", split_axis=0, concat_axis=0, tiled=True)

    wide_cos = cos_table.astype(np.float32)
    wide_sin = sin_table.astype(np.float32)
    backward = np.stack(
        [
            np.concatenate([wide_cos, -wide_sin], axis=1),
            np.concatenate([wide_sin, wide_cos], axis=1),
        ],
        axis=1,
    ).reshape(2 * ENERGIES, 2 * ENERGIES)
    result = pl.pallas_call(
        back_kernel,
        in_specs=[VMEM_SPEC] * 2,
        out_specs=VMEM_SPEC,
        out_shape=jax.ShapeDtypeStruct((2 * ENERGIES, PAIR), BF16),
        name="back",
    )(returned.reshape(ENERGIES, 2 * PAIR), jnp.asarray(backward, dtype=BF16))
    return result.reshape(1, ENERGIES, 1, 2, PAIR)


def solution(mesh):
    in_specs = (
        P("mom", "shard", None, None, None, None),
        P(),
        P("mom", "shard"),
        P(),
        P(),
        P("shard", None, None, None),
        P(),
        P(),
    )
    out_specs = P("mom", None, "shard", None, None)
    return jax.shard_map(local, mesh=mesh, in_specs=in_specs, out_specs=out_specs, check_vma=False)
```

```python
import jax
import jax.numpy as jnp
import numpy as np
from jax import lax
from jax.experimental import pallas as pl
from jax.experimental.pallas import tpu as pltpu
from jax.sharding import PartitionSpec as P

NORB = 16
ATL = 8
NBR = 4
ENERGIES = 256
LAYERS = 8
ORB = 128
PAIR = 256
ATOMS = 64
KPTS = 8
STEP_LAYERS = 2

F32 = jnp.float32
BF16 = jnp.bfloat16
VMEM_SPEC = pl.BlockSpec(memory_space=pltpu.VMEM)


def dft_tables(length):
    counter = np.arange(length)
    angles = (counter[:, None] * counter[None, :] % length) * (2.0 * np.pi / length)
    return np.cos(angles).astype(jnp.bfloat16), np.sin(angles).astype(jnp.bfloat16)


def pairs_kernel(occ_ref, nbr_ref, orb_ref, green_ref, broad_ref, out_ref, mix_ref):
    step = pl.program_id(0)
    energies = green_ref.shape[1]
    layers = green_ref.shape[2]

    @pl.when(step == 0)
    def _():
        mix_ref[:ORB, :ORB] = broad_ref[0]
        mix_ref[:ORB, ORB:] = broad_ref[1]
        mix_ref[ORB:, :ORB] = -broad_ref[1]
        mix_ref[ORB:, ORB:] = broad_ref[0]

    lane = lax.broadcasted_iota(jnp.int32, (1, ORB), 1)
    slot = (lane // NORB) % NBR
    column = lane % NORB
    source = lax.broadcasted_iota(jnp.int32, (ORB, ORB), 0)
    row = lax.broadcasted_iota(jnp.int32, (energies * NORB, ORB), 0) % NORB
    low = lax.broadcasted_iota(jnp.int32, (energies * NORB, ORB), 1) < ORB // 2
    for l in range(layers):
        rows = []
        for e in range(energies):
            rows.append(jnp.concatenate([green_ref[0, e, l, 0], green_ref[0, e, l, 1]], axis=1))
        left = jnp.dot(jnp.concatenate(rows, axis=0), mix_ref[...], preferred_element_type=F32)
        left = left.astype(BF16)
        full = []
        for e in range(energies):
            green_re = green_ref[0, e, l, 0]
            green_im = green_ref[0, e, l, 1]
            partner = jnp.concatenate(
                [
                    jnp.concatenate([green_re, green_im], axis=1),
                    jnp.concatenate([-green_im, green_re], axis=1),
                ],
                axis=0,
            )
            block = lax.dot_general(
                left[e * ORB : (e + 1) * ORB],
                partner,
                (((1,), (1,)), ((), ())),
                preferred_element_type=F32,
            )
            full.append((block * occ_ref[0, e]).astype(BF16))
        for a in range(ATL):
            atom = (step * layers + l) * ATL + a
            target = jnp.full((1, ORB), -1, jnp.int32)
            for n in range(NBR):
                partner_atom = nbr_ref[n, atom]
                start = (partner_atom % ATL) * NORB
                chosen = (slot == n) & (column < orb_ref[partner_atom])
                target = jnp.where(chosen, start + column, target)
            select = jnp.where(source == target, 1.0, 0.0).astype(BF16)
            part_rows = [
                full[e][a * NORB : (a + 1) * NORB, p * ORB : (p + 1) * ORB]
                for p in range(2)
                for e in range(energies)
            ]
            picked = jnp.dot(
                jnp.concatenate(part_rows, axis=0), select, preferred_element_type=F32
            )
            half = energies * NORB
            merged = jnp.where(low, picked[:half], picked[half:])
            merged = jnp.where(row < orb_ref[atom], merged, 0.0).astype(BF16)
            out_ref[l * ATL + a] = merged.reshape(energies, NORB, ORB)


def make_pairs(green_ret, broadening, occupation, neighbours, orbitals):
    energies = green_ret.shape[1]
    smem = pl.BlockSpec(memory_space=pltpu.SMEM)
    return pl.pallas_call(
        pairs_kernel,
        grid=(LAYERS // STEP_LAYERS,),
        in_specs=[
            smem,
            smem,
            smem,
            pl.BlockSpec((1, energies, STEP_LAYERS, 2, ORB, ORB), lambda s: (0, 0, s, 0, 0, 0)),
            pl.BlockSpec((2, ORB, ORB), lambda s: (0, 0, 0)),
        ],
        out_specs=pl.BlockSpec((STEP_LAYERS * ATL, energies, NORB, ORB), lambda s: (s, 0, 0, 0)),
        out_shape=jax.ShapeDtypeStruct((ATOMS, energies, NORB, ORB), BF16),
        scratch_shapes=[pltpu.VMEM((2 * ORB, 2 * ORB), BF16)],
        name="pairs",
    )(occupation, neighbours.T, orbitals, green_ret, broadening)


def couple_kernel(arrived_ref, weight_ref, mask_ref, table_ref, out_ref, wide):
    wide[...] = arrived_ref[...].reshape(ENERGIES * NORB, ORB).astype(F32)
    rows = [wide[pl.ds(i, ENERGIES, stride=NORB), :].astype(BF16) for i in range(NORB)]
    total = jnp.dot(
        jnp.concatenate(rows, axis=1), weight_ref[...], preferred_element_type=F32
    )
    coupled = (total * mask_ref[...]).astype(BF16)
    spectra = jnp.dot(table_ref[...], coupled, preferred_element_type=F32)
    out_ref[:, :PAIR] = (spectra[:ENERGIES, :PAIR] + spectra[ENERGIES:, PAIR:]).astype(BF16)
    out_ref[:, PAIR:] = (spectra[:ENERGIES, PAIR:] - spectra[ENERGIES:, :PAIR]).astype(BF16)


def convolve_kernel(values_ref, high_ref, low_ref, out_ref):
    for block in range(high_ref.shape[0]):
        times = slice(block * NORB, (block + 1) * NORB)
        values = jnp.concatenate(
            [
                values_ref[k, times, p * PAIR : (p + 1) * PAIR]
                for p in range(2)
                for k in range(KPTS)
            ],
            axis=0,
        )
        sums = jnp.dot(high_ref[block], values, preferred_element_type=F32) + jnp.dot(
            low_ref[block], values, preferred_element_type=F32
        )
        for k in range(KPTS):
            for p in range(2):
                first = (k * 2 + p) * NORB
                out_ref[k, times, p * PAIR : (p + 1) * PAIR] = sums[first : first + NORB].astype(
                    BF16
                )


def back_kernel(values_ref, table_ref, out_ref):
    values = jnp.concatenate([values_ref[:, :PAIR], values_ref[:, PAIR:]], axis=0)
    result = jnp.dot(table_ref[...], values, preferred_element_type=F32)
    result = (result * (1.0 / ENERGIES)).astype(BF16)
    out_ref[0, :, 0] = result.reshape(ENERGIES, 2, PAIR)


def in_vmem(value):
    return pltpu.with_memory_space_constraint(value, pltpu.VMEM)


def local(
    green_ret, broadening, occupation, neighbours, orbitals, coupling, phonon, mode_table
):
    highest = lax.Precision.HIGHEST
    pairs = make_pairs(green_ret, broadening, occupation, neighbours, orbitals)
    arrived = lax.all_to_all(pairs, "shard", split_axis=0, concat_axis=0, tiled=True)

    parts = coupling.reshape(NBR, NORB, NORB, PAIR).transpose(1, 0, 2, 3)
    parts = parts.reshape(NORB, NBR * NORB, PAIR)
    zeros = jnp.zeros_like(parts)
    weights = jnp.concatenate(
        [
            jnp.concatenate([parts, zeros], axis=2),
            jnp.concatenate([zeros, parts], axis=2),
        ],
        axis=1,
    ).reshape(2 * NBR * PAIR, 2 * PAIR)
    own_atom = lax.axis_index("shard")
    own_count = lax.dynamic_slice_in_dim(orbitals, own_atom, 1)[0]
    pair_index = jnp.arange(2 * PAIR, dtype=jnp.int32) % PAIR
    own_mask = (pair_index // NORB < own_count) & (pair_index % NORB < own_count)
    own_mask = own_mask.astype(F32)[None, :]
    cos_table, sin_table = dft_tables(ENERGIES)
    forward = jnp.asarray(np.concatenate([cos_table, sin_table], axis=0))
    timed = pl.pallas_call(
        couple_kernel,
        in_specs=[VMEM_SPEC] * 4,
        out_specs=VMEM_SPEC,
        out_shape=pltpu.VMEM((ENERGIES, 2 * PAIR), BF16),
        scratch_shapes=[pltpu.VMEM((ENERGIES * NORB, ORB), F32)],
        compiler_params=pltpu.CompilerParams(vmem_limit_bytes=24 * 2**20),
        name="couple",
    )(in_vmem(arrived), in_vmem(weights), in_vmem(own_mask), in_vmem(forward))

    span = ENERGIES // KPTS
    own_momentum = lax.axis_index("mom")
    own_phonon = lax.dynamic_slice_in_dim(phonon, own_momentum * span, span, 2)
    mode_ids = jnp.arange(phonon.shape[0], dtype=jnp.int32)
    one_hot = (mode_table.reshape(-1, 1) == mode_ids[None, :]).astype(F32)
    kernel = jnp.dot(one_hot, own_phonon.reshape(phonon.shape[0], -1), precision=highest)
    kernel = kernel.reshape(KPTS, KPTS, 2, span // NORB, NORB)
    kernel_re = kernel[:, :, 0].transpose(2, 0, 3, 1)
    kernel_im = kernel[:, :, 1].transpose(2, 0, 3, 1)
    terms = jnp.stack(
        [
            jnp.stack([kernel_re, -kernel_im], axis=3),
            jnp.stack([kernel_im, kernel_re], axis=3),
        ],
        axis=2,
    )
    same = jnp.eye(NORB, dtype=F32)[:, None, None, :]
    kernels = (terms[..., None] * same).reshape(span // NORB, 2 * KPTS * NORB, 2 * KPTS * NORB)
    high = kernels.astype(BF16)
    low = (kernels - high.astype(F32)).astype(BF16)

    moved = lax.all_to_all(
        timed.reshape(KPTS, span, 2 * PAIR), "mom", split_axis=0, concat_axis=0, tiled=True
    )
    convolved = pl.pallas_call(
        convolve_kernel,
        in_specs=[VMEM_SPEC] * 3,
        out_specs=VMEM_SPEC,
        out_shape=pltpu.VMEM((KPTS, span, 2 * PAIR), BF16),
        compiler_params=pltpu.CompilerParams(vmem_limit_bytes=12 * 2**20),
        name="convolve",
    )(in_vmem(moved), in_vmem(high), in_vmem(low))
    returned = lax.all_to_all(convolved, "mom", split_axis=0, concat_axis=0, tiled=True)

    wide_cos = cos_table.astype(np.float32)
    wide_sin = sin_table.astype(np.float32)
    backward = np.stack(
        [
            np.concatenate([wide_cos, -wide_sin], axis=1),
            np.concatenate([wide_sin, wide_cos], axis=1),
        ],
        axis=1,
    ).reshape(2 * ENERGIES, 2 * ENERGIES)
    return pl.pallas_call(
        back_kernel,
        in_specs=[VMEM_SPEC] * 2,
        out_specs=VMEM_SPEC,
        out_shape=jax.ShapeDtypeStruct((1, ENERGIES, 1, 2, PAIR), BF16),
        compiler_params=pltpu.CompilerParams(vmem_limit_bytes=12 * 2**20),
        name="back",
    )(in_vmem(returned.reshape(ENERGIES, 2 * PAIR)), in_vmem(jnp.asarray(backward, dtype=BF16)))


def solution(mesh):
    in_specs = (
        P("mom", "shard", None, None, None, None),
        P(),
        P("mom", "shard"),
        P(),
        P(),
        P("shard", None, None, None),
        P(),
        P(),
    )
    out_specs = P("mom", None, "shard", None, None)
    return jax.shard_map(local, mesh=mesh, in_specs=in_specs, out_specs=out_specs, check_vma=False)
```

```python
import jax
import jax.numpy as jnp
import numpy as np
from jax import lax
from jax.experimental import pallas as pl
from jax.experimental.pallas import tpu as pltpu
from jax.sharding import PartitionSpec as P

NORB = 16
ATL = 8
NBR = 4
ENERGIES = 256
LAYERS = 8
ORB = 128
PAIR = 256
ATOMS = 64
KPTS = 8
STEP_LAYERS = 4

F32 = jnp.float32
BF16 = jnp.bfloat16
VMEM_SPEC = pl.BlockSpec(memory_space=pltpu.VMEM)


def dft_tables(length):
    counter = np.arange(length)
    angles = (counter[:, None] * counter[None, :] % length) * (2.0 * np.pi / length)
    return np.cos(angles).astype(jnp.bfloat16), np.sin(angles).astype(jnp.bfloat16)


def pairs_kernel(occ_ref, nbr_ref, green_ref, broad_ref, out_ref, mix_ref, left_ref, full_ref):
    step = pl.program_id(0)
    energies = green_ref.shape[1]
    layers = green_ref.shape[2]

    @pl.when(step == 0)
    def _():
        mix_ref[:ORB, :ORB] = broad_ref[0]
        mix_ref[:ORB, ORB:] = broad_ref[1]
        mix_ref[ORB:, :ORB] = -broad_ref[1]
        mix_ref[ORB:, ORB:] = broad_ref[0]

    rows = [
        jnp.concatenate([green_ref[0, e, l, 0], green_ref[0, e, l, 1]], axis=1)
        for l in range(layers)
        for e in range(energies)
    ]
    left = jnp.dot(jnp.concatenate(rows, axis=0), mix_ref[...], preferred_element_type=F32)
    left_ref[...] = left.astype(BF16)
    for l in range(layers):
        for e in range(energies):
            block = slice((l * energies + e) * ORB, (l * energies + e + 1) * ORB)
            green_re = green_ref[0, e, l, 0]
            green_im = green_ref[0, e, l, 1]
            partner = jnp.concatenate(
                [
                    jnp.concatenate([green_re, green_im], axis=1),
                    jnp.concatenate([-green_im, green_re], axis=1),
                ],
                axis=0,
            )
            product = lax.dot_general(
                left_ref[block], partner, (((1,), (1,)), ((), ())), preferred_element_type=F32
            )
            full_ref[block] = (product * occ_ref[0, e]).astype(BF16)

    lane = lax.broadcasted_iota(jnp.int32, (1, ORB), 1)
    slot = (lane // NORB) % NBR
    column = lane % NORB
    source = lax.broadcasted_iota(jnp.int32, (ORB, ORB), 0).astype(F32).astype(BF16)
    half = energies * NORB
    low = lax.broadcasted_iota(jnp.int32, (half, ORB), 1) < ORB // 2
    one = jnp.ones((ORB, ORB), BF16)
    zero = jnp.zeros((ORB, ORB), BF16)
    for l in range(layers):
        for a in range(ATL):
            atom = (step * layers + l) * ATL + a
            starts = [(nbr_ref[n, atom] & (ATL - 1)) * NORB for n in range(NBR)]
            target = jnp.where(
                slot < 2,
                jnp.where(slot == 0, starts[0], starts[1]),
                jnp.where(slot == 2, starts[2], starts[3]),
            )
            target = (target + column).astype(F32).astype(BF16)
            select = jnp.where(source == target, one, zero)
            part_rows = [
                full_ref[
                    (l * energies + e) * ORB + a * NORB : (l * energies + e) * ORB + (a + 1) * NORB,
                    p * ORB : (p + 1) * ORB,
                ]
                for p in range(2)
                for e in range(energies)
            ]
            picked = jnp.dot(
                jnp.concatenate(part_rows, axis=0), select, preferred_element_type=F32
            )
            merged = jnp.where(low, picked[:half], picked[half:]).astype(BF16)
            out_ref[l * ATL + a] = merged.reshape(energies, NORB, ORB)


def make_pairs(green_ret, broadening, occupation, neighbours):
    energies = green_ret.shape[1]
    smem = pl.BlockSpec(memory_space=pltpu.SMEM)
    rows = STEP_LAYERS * energies * ORB
    return pl.pallas_call(
        pairs_kernel,
        grid=(LAYERS // STEP_LAYERS,),
        in_specs=[
            smem,
            smem,
            pl.BlockSpec((1, energies, STEP_LAYERS, 2, ORB, ORB), lambda s: (0, 0, s, 0, 0, 0)),
            pl.BlockSpec((2, ORB, ORB), lambda s: (0, 0, 0)),
        ],
        out_specs=pl.BlockSpec((STEP_LAYERS * ATL, energies, NORB, ORB), lambda s: (s, 0, 0, 0)),
        out_shape=jax.ShapeDtypeStruct((ATOMS, energies, NORB, ORB), BF16),
        scratch_shapes=[
            pltpu.VMEM((2 * ORB, 2 * ORB), BF16),
            pltpu.VMEM((rows, 2 * ORB), BF16),
            pltpu.VMEM((rows, 2 * ORB), BF16),
        ],
        name="pairs",
    )(occupation, neighbours.T, green_ret, broadening)


def couple_kernel(arrived_ref, weight_ref, table_hbm, out_ref, wide, table_ref, table_sem):
    table_copy = pltpu.make_async_copy(table_hbm, table_ref, table_sem)
    table_copy.start()
    wide[...] = arrived_ref[...].reshape(ENERGIES * NORB, ORB).astype(F32)
    rows = [wide[pl.ds(i, ENERGIES, stride=NORB), :].astype(BF16) for i in range(NORB)]
    total = jnp.dot(
        jnp.concatenate(rows, axis=1), weight_ref[...], preferred_element_type=F32
    )
    coupled = total.astype(BF16)
    table_copy.wait()
    spectra = jnp.dot(table_ref[...], coupled, preferred_element_type=F32)
    out_ref[:, :PAIR] = (spectra[:ENERGIES, :PAIR] + spectra[ENERGIES:, PAIR:]).astype(BF16)
    out_ref[:, PAIR:] = (spectra[:ENERGIES, PAIR:] - spectra[ENERGIES:, :PAIR]).astype(BF16)


def convolve_kernel(values_ref, high_ref, low_ref, out_ref):
    for block in range(high_ref.shape[0]):
        times = slice(block * NORB, (block + 1) * NORB)
        values = jnp.concatenate(
            [
                values_ref[k, times, p * PAIR : (p + 1) * PAIR]
                for p in range(2)
                for k in range(KPTS)
            ],
            axis=0,
        )
        sums = jnp.dot(high_ref[block], values, preferred_element_type=F32) + jnp.dot(
            low_ref[block], values, preferred_element_type=F32
        )
        for k in range(KPTS):
            for p in range(2):
                first = (k * 2 + p) * NORB
                out_ref[k, times, p * PAIR : (p + 1) * PAIR] = sums[first : first + NORB].astype(
                    BF16
                )


def back_kernel(values_ref, table_ref, out_ref):
    values = jnp.concatenate([values_ref[:, :PAIR], values_ref[:, PAIR:]], axis=0)
    result = jnp.dot(table_ref[...], values, preferred_element_type=F32)
    result = (result * (1.0 / ENERGIES)).astype(BF16)
    out_ref[0, :, 0] = result.reshape(ENERGIES, 2, PAIR)


def in_vmem(value):
    return pltpu.with_memory_space_constraint(value, pltpu.VMEM)


def in_hbm(value):
    return pltpu.with_memory_space_constraint(value, pltpu.HBM)


def local(
    green_ret, broadening, occupation, neighbours, orbitals, coupling, phonon, mode_table
):
    highest = lax.Precision.HIGHEST
    pairs = make_pairs(green_ret, broadening, occupation, neighbours)
    arrived = lax.all_to_all(pairs, "shard", split_axis=0, concat_axis=0, tiled=True)

    own_atom = lax.axis_index("shard")
    own_count = lax.dynamic_slice_in_dim(orbitals, own_atom, 1)[0]
    own_slots = lax.dynamic_slice_in_dim(neighbours, own_atom, 1)[0]
    slot_atoms = own_slots[:, None] == jnp.arange(ATOMS, dtype=jnp.int32)[None, :]
    slot_counts = jnp.sum(jnp.where(slot_atoms, orbitals[None, :], 0), axis=1)
    counter = jnp.arange(NORB, dtype=jnp.int32)
    pair_index = jnp.arange(PAIR, dtype=jnp.int32)
    own_mask = (pair_index // NORB < own_count) & (pair_index % NORB < own_count)
    keep = (
        (counter < own_count)[:, None, None, None]
        & (counter[None, :] < slot_counts[:, None])[None, :, :, None]
        & own_mask[None, None, None, :]
    )
    parts = coupling.reshape(NBR, NORB, NORB, PAIR).transpose(1, 0, 2, 3)
    parts = jnp.where(keep, parts, jnp.zeros_like(parts)).reshape(NORB, NBR * NORB, PAIR)
    zeros = jnp.zeros_like(parts)
    weights = jnp.concatenate(
        [
            jnp.concatenate([parts, zeros], axis=2),
            jnp.concatenate([zeros, parts], axis=2),
        ],
        axis=1,
    ).reshape(2 * NBR * PAIR, 2 * PAIR)
    span = ENERGIES // KPTS
    own_momentum = lax.axis_index("mom")
    own_phonon = lax.dynamic_slice_in_dim(phonon, own_momentum * span, span, 2)
    mode_ids = jnp.arange(phonon.shape[0], dtype=jnp.int32)
    one_hot = (mode_table.reshape(-1, 1) == mode_ids[None, :]).astype(F32)
    kernel = jnp.dot(one_hot, own_phonon.reshape(phonon.shape[0], -1), precision=highest)
    kernel = kernel.reshape(KPTS, KPTS, 2, span // NORB, NORB)
    kernel_re = kernel[:, :, 0].transpose(2, 0, 3, 1)
    kernel_im = kernel[:, :, 1].transpose(2, 0, 3, 1)
    terms = jnp.stack(
        [
            jnp.stack([kernel_re, -kernel_im], axis=3),
            jnp.stack([kernel_im, kernel_re], axis=3),
        ],
        axis=2,
    )
    same = jnp.eye(NORB, dtype=F32)[:, None, None, :]
    kernels = (terms[..., None] * same).reshape(span // NORB, 2 * KPTS * NORB, 2 * KPTS * NORB)
    high = kernels.astype(BF16)
    low = (kernels - high.astype(F32)).astype(BF16)
    cos_table, sin_table = dft_tables(ENERGIES)
    forward = np.concatenate([cos_table, sin_table], axis=0)
    wide_cos = cos_table.astype(np.float32)
    wide_sin = sin_table.astype(np.float32)
    backward = np.stack(
        [
            np.concatenate([wide_cos, -wide_sin], axis=1),
            np.concatenate([wide_sin, wide_cos], axis=1),
        ],
        axis=1,
    ).reshape(2 * ENERGIES, 2 * ENERGIES)
    arrived, weights, high, low = lax.optimization_barrier((arrived, weights, high, low))
    timed = pl.pallas_call(
        couple_kernel,
        in_specs=[VMEM_SPEC, VMEM_SPEC, pl.BlockSpec(memory_space=pltpu.HBM)],
        out_specs=VMEM_SPEC,
        out_shape=pltpu.VMEM((ENERGIES, 2 * PAIR), BF16),
        scratch_shapes=[
            pltpu.VMEM((ENERGIES * NORB, ORB), F32),
            pltpu.VMEM((2 * ENERGIES, ENERGIES), BF16),
            pltpu.SemaphoreType.DMA,
        ],
        compiler_params=pltpu.CompilerParams(vmem_limit_bytes=24 * 2**20),
        name="couple",
    )(in_vmem(arrived), in_vmem(weights), in_hbm(jnp.asarray(forward)))

    moved = lax.all_to_all(
        timed.reshape(KPTS, span, 2 * PAIR), "mom", split_axis=0, concat_axis=0, tiled=True
    )
    convolved = pl.pallas_call(
        convolve_kernel,
        in_specs=[VMEM_SPEC] * 3,
        out_specs=VMEM_SPEC,
        out_shape=pltpu.VMEM((KPTS, span, 2 * PAIR), BF16),
        compiler_params=pltpu.CompilerParams(vmem_limit_bytes=12 * 2**20),
        name="convolve",
    )(in_vmem(moved), in_vmem(high), in_vmem(low))
    returned = lax.all_to_all(convolved, "mom", split_axis=0, concat_axis=0, tiled=True)

    return pl.pallas_call(
        back_kernel,
        in_specs=[VMEM_SPEC] * 2,
        out_specs=VMEM_SPEC,
        out_shape=jax.ShapeDtypeStruct((1, ENERGIES, 1, 2, PAIR), BF16),
        compiler_params=pltpu.CompilerParams(vmem_limit_bytes=12 * 2**20),
        name="back",
    )(in_vmem(returned.reshape(ENERGIES, 2 * PAIR)), in_vmem(jnp.asarray(backward, dtype=BF16)))


def solution(mesh):
    in_specs = (
        P("mom", "shard", None, None, None, None),
        P(),
        P("mom", "shard"),
        P(),
        P(),
        P("shard", None, None, None),
        P(),
        P(),
    )
    out_specs = P("mom", None, "shard", None, None)
    return jax.shard_map(local, mesh=mesh, in_specs=in_specs, out_specs=out_specs, check_vma=False)
```

```python
import jax
import jax.numpy as jnp
import numpy as np
from jax import lax
from jax.experimental import pallas as pl
from jax.experimental.pallas import tpu as pltpu
from jax.sharding import PartitionSpec as P

NORB = 16
ATL = 8
NBR = 4
ENERGIES = 256
LAYERS = 8
ORB = 128
PAIR = 256
ATOMS = 64
KPTS = 8
STEP_LAYERS = 4

F32 = jnp.float32
BF16 = jnp.bfloat16
VMEM_SPEC = pl.BlockSpec(memory_space=pltpu.VMEM)


def dft_tables(length):
    counter = lax.optimization_barrier(jnp.arange(length, dtype=jnp.int32))
    phases = counter[:, None] * counter[None, :] % length
    angles = phases.astype(F32) * (2.0 * np.pi / length)
    return jnp.cos(angles).astype(BF16), jnp.sin(angles).astype(BF16)


def pairs_kernel(occ_ref, nbr_ref, green_ref, broad_ref, out_ref, mix_ref, left_ref, full_ref):
    step = pl.program_id(0)
    energies = green_ref.shape[1]
    layers = green_ref.shape[2]

    @pl.when(step == 0)
    def _():
        mix_ref[:ORB, :ORB] = broad_ref[0]
        mix_ref[:ORB, ORB:] = broad_ref[1]
        mix_ref[ORB:, :ORB] = -broad_ref[1]
        mix_ref[ORB:, ORB:] = broad_ref[0]

    rows = [
        jnp.concatenate([green_ref[0, e, l, 0], green_ref[0, e, l, 1]], axis=1)
        for l in range(layers)
        for e in range(energies)
    ]
    left = jnp.dot(jnp.concatenate(rows, axis=0), mix_ref[...], preferred_element_type=F32)
    left_ref[...] = left.astype(BF16)
    for l in range(layers):
        for e in range(energies):
            block = slice((l * energies + e) * ORB, (l * energies + e + 1) * ORB)
            green_re = green_ref[0, e, l, 0]
            green_im = green_ref[0, e, l, 1]
            partner = jnp.concatenate(
                [
                    jnp.concatenate([green_re, green_im], axis=1),
                    jnp.concatenate([-green_im, green_re], axis=1),
                ],
                axis=0,
            )
            product = lax.dot_general(
                left_ref[block], partner, (((1,), (1,)), ((), ())), preferred_element_type=F32
            )
            full_ref[block] = (product * occ_ref[0, e]).astype(BF16)

    lane = lax.broadcasted_iota(jnp.int32, (1, ORB), 1)
    slot = (lane // NORB) % NBR
    column = lane % NORB
    source = lax.broadcasted_iota(jnp.int32, (ORB, ORB), 0).astype(F32).astype(BF16)
    half = energies * NORB
    low = lax.broadcasted_iota(jnp.int32, (half, ORB), 1) < ORB // 2
    one = jnp.ones((ORB, ORB), BF16)
    zero = jnp.zeros((ORB, ORB), BF16)
    for l in range(layers):
        for a in range(ATL):
            atom = (step * layers + l) * ATL + a
            starts = [(nbr_ref[n, atom] & (ATL - 1)) * NORB for n in range(NBR)]
            target = jnp.where(
                slot < 2,
                jnp.where(slot == 0, starts[0], starts[1]),
                jnp.where(slot == 2, starts[2], starts[3]),
            )
            target = (target + column).astype(F32).astype(BF16)
            select = jnp.where(source == target, one, zero)
            part_rows = [
                full_ref[
                    (l * energies + e) * ORB + a * NORB : (l * energies + e) * ORB + (a + 1) * NORB,
                    p * ORB : (p + 1) * ORB,
                ]
                for p in range(2)
                for e in range(energies)
            ]
            picked = jnp.dot(
                jnp.concatenate(part_rows, axis=0), select, preferred_element_type=F32
            )
            merged = jnp.where(low, picked[:half], picked[half:]).astype(BF16)
            out_ref[l * ATL + a] = merged.reshape(energies, NORB, ORB)


def make_pairs(green_ret, broadening, occupation, neighbours):
    energies = green_ret.shape[1]
    smem = pl.BlockSpec(memory_space=pltpu.SMEM)
    rows = STEP_LAYERS * energies * ORB
    return pl.pallas_call(
        pairs_kernel,
        grid=(LAYERS // STEP_LAYERS,),
        in_specs=[
            smem,
            smem,
            pl.BlockSpec((1, energies, STEP_LAYERS, 2, ORB, ORB), lambda s: (0, 0, s, 0, 0, 0)),
            pl.BlockSpec((2, ORB, ORB), lambda s: (0, 0, 0)),
        ],
        out_specs=pl.BlockSpec((STEP_LAYERS * ATL, energies, NORB, ORB), lambda s: (s, 0, 0, 0)),
        out_shape=jax.ShapeDtypeStruct((ATOMS, energies, NORB, ORB), BF16),
        scratch_shapes=[
            pltpu.VMEM((2 * ORB, 2 * ORB), BF16),
            pltpu.VMEM((rows, 2 * ORB), BF16),
            pltpu.VMEM((rows, 2 * ORB), BF16),
        ],
        name="pairs",
    )(occupation, neighbours.T, green_ret, broadening)


def couple_kernel(arrived_ref, weight_ref, table_ref, out_ref, wide):
    wide[...] = arrived_ref[...].reshape(ENERGIES * NORB, ORB).astype(F32)
    rows = [wide[pl.ds(i, ENERGIES, stride=NORB), :].astype(BF16) for i in range(NORB)]
    total = jnp.dot(
        jnp.concatenate(rows, axis=1), weight_ref[...], preferred_element_type=F32
    )
    coupled = total.astype(BF16)
    spectra = jnp.dot(table_ref[...], coupled, preferred_element_type=F32)
    out_ref[:, :PAIR] = (spectra[:ENERGIES, :PAIR] + spectra[ENERGIES:, PAIR:]).astype(BF16)
    out_ref[:, PAIR:] = (spectra[:ENERGIES, PAIR:] - spectra[ENERGIES:, :PAIR]).astype(BF16)


def convolve_kernel(values_ref, high_ref, low_ref, out_ref):
    for block in range(high_ref.shape[0]):
        times = slice(block * NORB, (block + 1) * NORB)
        values = jnp.concatenate(
            [
                values_ref[k, times, p * PAIR : (p + 1) * PAIR]
                for p in range(2)
                for k in range(KPTS)
            ],
            axis=0,
        )
        sums = jnp.dot(high_ref[block], values, preferred_element_type=F32) + jnp.dot(
            low_ref[block], values, preferred_element_type=F32
        )
        for k in range(KPTS):
            for p in range(2):
                first = (k * 2 + p) * NORB
                out_ref[k, times, p * PAIR : (p + 1) * PAIR] = sums[first : first + NORB].astype(
                    BF16
                )


def back_kernel(values_ref, table_ref, out_ref):
    values = jnp.concatenate([values_ref[:, :PAIR], values_ref[:, PAIR:]], axis=0)
    result = jnp.dot(table_ref[...], values, preferred_element_type=F32)
    result = (result * (1.0 / ENERGIES)).astype(BF16)
    out_ref[0, :, 0] = result.reshape(ENERGIES, 2, PAIR)


def in_vmem(value):
    return pltpu.with_memory_space_constraint(value, pltpu.VMEM)


def local(
    green_ret, broadening, occupation, neighbours, orbitals, coupling, phonon, mode_table
):
    highest = lax.Precision.HIGHEST
    pairs = make_pairs(green_ret, broadening, occupation, neighbours)
    arrived = lax.all_to_all(pairs, "shard", split_axis=0, concat_axis=0, tiled=True)

    own_atom = lax.axis_index("shard")
    own_count = lax.dynamic_slice_in_dim(orbitals, own_atom, 1)[0]
    own_slots = lax.dynamic_slice_in_dim(neighbours, own_atom, 1)[0]
    slot_atoms = own_slots[:, None] == jnp.arange(ATOMS, dtype=jnp.int32)[None, :]
    slot_counts = jnp.sum(jnp.where(slot_atoms, orbitals[None, :], 0), axis=1)
    counter = jnp.arange(NORB, dtype=jnp.int32)
    pair_index = jnp.arange(PAIR, dtype=jnp.int32)
    own_mask = (pair_index // NORB < own_count) & (pair_index % NORB < own_count)
    keep = (
        (counter < own_count)[:, None, None, None]
        & (counter[None, :] < slot_counts[:, None])[None, :, :, None]
        & own_mask[None, None, None, :]
    )
    parts = coupling.reshape(NBR, NORB, NORB, PAIR).transpose(1, 0, 2, 3)
    parts = jnp.where(keep, parts, jnp.zeros_like(parts)).reshape(NORB, NBR * NORB, PAIR)
    zeros = jnp.zeros_like(parts)
    weights = jnp.concatenate(
        [
            jnp.concatenate([parts, zeros], axis=2),
            jnp.concatenate([zeros, parts], axis=2),
        ],
        axis=1,
    ).reshape(2 * NBR * PAIR, 2 * PAIR)
    span = ENERGIES // KPTS
    own_momentum = lax.axis_index("mom")
    own_phonon = lax.dynamic_slice_in_dim(phonon, own_momentum * span, span, 2)
    mode_ids = jnp.arange(phonon.shape[0], dtype=jnp.int32)
    one_hot = (mode_table.reshape(-1, 1) == mode_ids[None, :]).astype(F32)
    kernel = jnp.dot(one_hot, own_phonon.reshape(phonon.shape[0], -1), precision=highest)
    kernel = kernel.reshape(KPTS, KPTS, 2, span // NORB, NORB)
    kernel_re = kernel[:, :, 0].transpose(2, 0, 3, 1)
    kernel_im = kernel[:, :, 1].transpose(2, 0, 3, 1)
    terms = jnp.stack(
        [
            jnp.stack([kernel_re, -kernel_im], axis=3),
            jnp.stack([kernel_im, kernel_re], axis=3),
        ],
        axis=2,
    )
    same = jnp.eye(NORB, dtype=F32)[:, None, None, :]
    kernels = (terms[..., None] * same).reshape(span // NORB, 2 * KPTS * NORB, 2 * KPTS * NORB)
    high = kernels.astype(BF16)
    low = (kernels - high.astype(F32)).astype(BF16)
    cos_table, sin_table = dft_tables(ENERGIES)
    forward = jnp.concatenate([cos_table, sin_table], axis=0)
    backward = jnp.stack(
        [
            jnp.concatenate([cos_table, -sin_table], axis=1),
            jnp.concatenate([sin_table, cos_table], axis=1),
        ],
        axis=1,
    ).reshape(2 * ENERGIES, 2 * ENERGIES)
    arrived, weights, high, low, forward, backward = lax.optimization_barrier(
        (arrived, weights, high, low, forward, backward)
    )
    timed = pl.pallas_call(
        couple_kernel,
        in_specs=[VMEM_SPEC] * 3,
        out_specs=VMEM_SPEC,
        out_shape=pltpu.VMEM((ENERGIES, 2 * PAIR), BF16),
        scratch_shapes=[pltpu.VMEM((ENERGIES * NORB, ORB), F32)],
        compiler_params=pltpu.CompilerParams(vmem_limit_bytes=24 * 2**20),
        name="couple",
    )(in_vmem(arrived), in_vmem(weights), in_vmem(forward))

    moved = lax.all_to_all(
        timed.reshape(KPTS, span, 2 * PAIR), "mom", split_axis=0, concat_axis=0, tiled=True
    )
    convolved = pl.pallas_call(
        convolve_kernel,
        in_specs=[VMEM_SPEC] * 3,
        out_specs=VMEM_SPEC,
        out_shape=pltpu.VMEM((KPTS, span, 2 * PAIR), BF16),
        compiler_params=pltpu.CompilerParams(vmem_limit_bytes=12 * 2**20),
        name="convolve",
    )(in_vmem(moved), in_vmem(high), in_vmem(low))
    returned = lax.all_to_all(convolved, "mom", split_axis=0, concat_axis=0, tiled=True)

    return pl.pallas_call(
        back_kernel,
        in_specs=[VMEM_SPEC] * 2,
        out_specs=VMEM_SPEC,
        out_shape=jax.ShapeDtypeStruct((1, ENERGIES, 1, 2, PAIR), BF16),
        compiler_params=pltpu.CompilerParams(vmem_limit_bytes=12 * 2**20),
        name="back",
    )(in_vmem(returned.reshape(ENERGIES, 2 * PAIR)), in_vmem(backward))


def solution(mesh):
    in_specs = (
        P("mom", "shard", None, None, None, None),
        P(),
        P("mom", "shard"),
        P(),
        P(),
        P("shard", None, None, None),
        P(),
        P(),
    )
    out_specs = P("mom", None, "shard", None, None)
    return jax.shard_map(local, mesh=mesh, in_specs=in_specs, out_specs=out_specs, check_vma=False)
```
